32 devices in a mesh: groups: 2 (over y), seq: 4 (over z), heads: 4 (over x, core).
Axes of the slice: x: 2, y: 2, z: 4, core: 2. Of those that a mesh axis runs over, the one named last changes fastest.
Arguments:
- queries: bfloat16 [4096, 24, 128], P(('groups', 'seq'), 'heads'), parts along dimension 0, may hold values from -130 to 130
- keys: bfloat16 [4096, 24, 128], P(('groups', 'seq'), 'heads'), parts along dimension 0, may hold values from -6 to 6
- values: bfloat16 [4096, 24, 128], P(('groups', 'seq'), 'heads'), parts along dimension 0, may hold values from -6 to 6
- pool_keys: bfloat16 [24, 8, 128], P('heads'), may hold values from -0.5 to 0.5
- pool_values: bfloat16 [24, 8, 128], P('heads'), may hold values from -0.5 to 0.5
Outputs:
- attended: bfloat16 [4096, 24, 128], P(('groups', 'seq'), 'heads'), parts along dimension 0
The draws below stay inside these ranges and needn't reach their ends.
There are 2 independent parts, one for each index of `groups`. The reference program is written for one: setup_inputs(seed, part) draws one part's arguments, and reference() takes and returns one part's arrays. A program takes and returns all parts, laid end to end along the dimension named above; an argument that names none is the same for every part. Nothing has to cross between parts.
All inputs are finite; a program needn't handle non-finite values.
Results may differ from the reference program's by a relative error of at most 0.01.
Values may be sent and summed in bfloat16 or wider, within the bound.
A program may use at most 64 MiB of HBM per device.

```python
import jax
import jax.numpy as jnp
from jax import lax

HD = 128
HEADS = 24
BLOCK = 128
SUMS = 8
TOKENS = 2048


def common_rows(key):
    base_keys = jnp.clip(jax.random.normal(jax.random.fold_in(key, 11), (TOKENS, HEADS, HD), jnp.float32), -6.0, 6.0)
    base_queries = jnp.clip(2.5 * jax.random.normal(jax.random.fold_in(key, 12), (TOKENS, HEADS, HD), jnp.float32), -15.0, 15.0)
    return (base_keys, base_queries)


def draw_keys(key, part):
    base_keys, base_queries = common_rows(key)
    return base_keys.astype(jnp.bfloat16)


def draw_queries(key, part):
    base_keys, base_queries = common_rows(key)
    return base_queries.astype(jnp.bfloat16)


def block_levels(key, dims, shards, smallest, top_value):
    gain = 1.0
    for position, shards_of in shards:
        draws = jax.random.uniform(jax.random.fold_in(jax.random.fold_in(key, 6), position), (shards_of,), jnp.float32, smallest / len(shards), top_value / len(shards))
        gain = gain * jnp.repeat(jnp.exp(draws), dims[position] // shards_of).reshape((-1,) + (1,) * (len(dims) - 1 - position))
    return gain


def normal_values(key, dims, width, reach, shards=(), kind=jnp.bfloat16):
    drawn = width * jax.random.normal(key, dims, jnp.float32)
    if shards:
        drawn = drawn * block_levels(key, dims, shards, -0.22, 0.18)
    return jnp.clip(drawn, -reach, reach).astype(kind)


def setup_inputs(seed: int = 0, part: int = 0) -> dict:
    key_list = jax.random.split(jax.random.key(seed), 6)
    own_keys = jax.random.split(jax.random.fold_in(key_list[5], part), 6)
    queries = draw_queries(jax.random.fold_in(jax.random.fold_in(key_list[5], part), 71), part)
    keys = draw_keys(jax.random.fold_in(jax.random.fold_in(key_list[5], part), 71), part)
    values = normal_values(own_keys[2], (TOKENS, HEADS, HD), 1.0, 6.0, ((0, 4), (1, 4)))
    pool_keys = normal_values(key_list[3], (HEADS, SUMS, BLOCK), BLOCK ** -0.5, 0.5, ((0, 4),))
    pool_values = normal_values(key_list[4], (HEADS, SUMS, BLOCK), BLOCK ** -0.5, 0.5, ((0, 4),))
    return {"queries": queries, "keys": keys, "values": values, "pool_keys": pool_keys, "pool_values": pool_values}


NEG = -1.0e30


def reference(queries, keys, values, pool_keys, pool_values):
    blocks = TOKENS // BLOCK
    logit_scale = HD ** -0.5
    key_blocks = keys.reshape(blocks, BLOCK, HEADS, HD).astype(jnp.float32)
    value_blocks = values.reshape(blocks, BLOCK, HEADS, HD).astype(jnp.float32)
    summary_keys = jnp.einsum("hsb,nbhd->nshd", pool_keys.astype(jnp.float32), key_blocks).astype(jnp.bfloat16).reshape(blocks * SUMS, HEADS, HD)
    summary_values = jnp.einsum("hsb,nbhd->nshd", pool_values.astype(jnp.float32), value_blocks).astype(jnp.bfloat16).reshape(blocks * SUMS, HEADS, HD)
    positions = jnp.arange(TOKENS, dtype=jnp.int32)
    query_block = positions // BLOCK
    row_block = jnp.arange(blocks * SUMS, dtype=jnp.int32) // SUMS
    summary_mask = row_block[None, :] < query_block[:, None]
    inner = jnp.arange(BLOCK, dtype=jnp.int32)[:, None]
    outer = jnp.arange(2 * BLOCK, dtype=jnp.int32)[None, :]
    block_index = jnp.arange(blocks, dtype=jnp.int32)[:, None, None]
    window_mask = ((outer > inner) & (outer <= inner + BLOCK))[None] & (block_index * BLOCK + outer[None] - BLOCK >= 0)

    def one_head(input_arrays):
        query_matrix, key_row_slab, value_row_slab, summary_key_rows, summary_value_rows = input_arrays
        padding = jnp.zeros((BLOCK, HD), jnp.bfloat16)
        key_ext = jnp.concatenate([padding, key_row_slab], axis=0).reshape(blocks + 1, BLOCK, HD)
        value_ext = jnp.concatenate([padding, value_row_slab], axis=0).reshape(blocks + 1, BLOCK, HD)
        key_win = jnp.concatenate([key_ext[:-1], key_ext[1:]], axis=1)
        value_win = jnp.concatenate([value_ext[:-1], value_ext[1:]], axis=1)
        query_blocks = query_matrix.reshape(blocks, BLOCK, HD)
        window_scores = jnp.einsum("nid,njd->nij", query_blocks.astype(jnp.float32), key_win.astype(jnp.float32)) * logit_scale
        window_scores = jnp.where(window_mask, window_scores, NEG)
        summary_logits = jnp.dot(query_matrix, summary_key_rows.T, preferred_element_type=jnp.float32) * logit_scale
        summary_logits = jnp.where(summary_mask, summary_logits, NEG)
        top = jnp.maximum(window_scores.max(-1).reshape(TOKENS), summary_logits.max(-1))
        window_weights = jnp.where(window_mask, jnp.exp(window_scores - top.reshape(blocks, BLOCK, 1)), 0.0)
        summary_weights = jnp.where(summary_mask, jnp.exp(summary_logits - top[:, None]), 0.0)
        total = window_weights.sum(-1).reshape(TOKENS) + summary_weights.sum(-1)
        window_b = lax.optimization_barrier(window_weights.astype(jnp.bfloat16))
        window_part = jnp.einsum("nij,njd->nid", window_b.astype(jnp.float32), value_win.astype(jnp.float32)).reshape(TOKENS, HD)
        summary_part = jnp.dot(summary_weights.astype(jnp.bfloat16), summary_value_rows, preferred_element_type=jnp.float32)
        return ((window_part + summary_part) / total[:, None]).astype(jnp.bfloat16)

    result = lax.map(one_head, (jnp.moveaxis(queries, 1, 0), jnp.moveaxis(keys, 1, 0), jnp.moveaxis(values, 1, 0), jnp.moveaxis(summary_keys, 1, 0), jnp.moveaxis(summary_values, 1, 0)))
    return jnp.moveaxis(result, 0, 1)
```

```python
import functools
import math

import jax
import jax.numpy as jnp
from jax import lax
from jax.experimental import pallas as pl
from jax.experimental.pallas import tpu as pltpu
from jax.sharding import PartitionSpec as P

NEG = -1e30
F32 = jnp.float32
BF16 = jnp.bfloat16


def dot_t(a, b):
    return lax.dot_general(a, b, (((1,), (1,)), ((), ())), preferred_element_type=F32)


def dot(a, b):
    return jnp.dot(a, b, preferred_element_type=F32)


def kernel(
    peers, span, q_hbm, k_hbm, v_hbm, pk_hbm, pv_hbm, o_ref,
    q_buf, k_buf, v_buf, pk_ref, pv_ref, last_vt, asked, answer, back, stat, stat_back,
    summ, top_s, total_s, acc_s,
    in_sem, pool_sem, ask_send, ask_recv, back_send, back_recv, stat_sem, sum_send, sum_recv,
):
    heads, rows, width = q_buf.shape
    sums, block = pk_ref.shape[1], pk_ref.shape[2]
    blocks = rows // block
    own = blocks * sums
    per = block // own
    slots = summ.shape[0]
    chunks = heads // span
    gain = (width ** -0.5) * math.log2(math.e)
    spot = lax.axis_index("seq")
    has_next = spot < peers - 1
    has_prev = spot > 0

    pools = [
        pltpu.make_async_copy(src, dst, pool_sem.at[i])
        for i, (src, dst) in enumerate(((pk_hbm, pk_ref), (pv_hbm, pv_ref)))
    ]
    for copy in pools:
        copy.start()

    def load(i, h):
        src, dst = ((k_hbm, k_buf), (v_hbm, v_buf), (q_hbm, q_buf))[i]
        return pltpu.make_async_copy(src.at[h], dst.at[h], in_sem.at[i, h])

    for h in range(heads):
        load(0, h).start()
        load(1, h).start()
    for h in range(heads):
        load(2, h).start()

    barrier = pltpu.get_barrier_semaphore()

    def greet(to):
        pl.semaphore_signal(
            barrier, inc=1, device_id={"seq": to}, device_id_type=pl.DeviceIdType.MESH
        )

    @pl.when(has_prev)
    def _():
        greet(spot - 1)

    @pl.when(has_next)
    def _():
        greet(spot + 1)

    def clear(i, c):
        summ[i] = jnp.zeros(summ.shape[1:], BF16)
        return c

    lax.fori_loop(spot + 1, slots, clear, 0)

    @pl.when(spot == 0)
    def _():
        back[...] = jnp.zeros(back.shape, BF16)
        top_row = lax.broadcasted_iota(jnp.int32, stat_back.shape, 1) == 0
        stat_back[...] = jnp.where(top_row, NEG, 0.0)

    pl.semaphore_wait(barrier, jnp.where(has_prev, 1, 0) + jnp.where(has_next, 1, 0))

    def remote(src, dst, send_sem, recv_sem, to):
        return pltpu.make_async_remote_copy(
            src_ref=src,
            dst_ref=dst,
            send_sem=send_sem,
            recv_sem=recv_sem,
            device_id={"seq": to},
            device_id_type=pl.DeviceIdType.MESH,
        )

    def ask(h, to):
        src = q_hbm.at[h, pl.ds(0, block), :]
        return remote(src, asked.at[h], ask_send.at[h], ask_recv.at[h], to)

    def give(h, to):
        return remote(answer.at[h], back.at[h], back_send.at[h], back_recv.at[h], to)

    def give_stat(h, to):
        return remote(stat.at[h], stat_back.at[h], stat_sem.at[0, h], stat_sem.at[1, h], to)

    def sum_copy(source, g, to):
        at = summ.at[source, pl.ds(g * span, span)]
        return remote(at, at, sum_send.at[source, g], sum_recv.at[source, g], to)

    @pl.when(has_prev)
    def _():
        for h in range(heads):
            ask(h, spot - 1).start()

    for copy in pools:
        copy.wait()
    for g in range(chunks):
        for h in range(g * span, (g + 1) * span):
            for which, (pool, buf) in enumerate(((pk_ref, k_buf), (pv_ref, v_buf))):
                load(which, h).wait()
                parts = [dot(pool[h], buf[h, b * block : (b + 1) * block]) for b in range(blocks)]
                summ[spot, h, which] = jnp.concatenate(parts, axis=0).astype(BF16)

        @pl.when(has_next)
        def _():
            sum_copy(spot, g, spot + 1).start()

    for h in range(heads):
        load(2, h).wait()

    key_at = lax.broadcasted_iota(jnp.int32, (block, block), 0)
    query_at = lax.broadcasted_iota(jnp.int32, (block, block), 1)
    here = key_at <= query_at

    def span_of(b, n=1):
        return pl.ds(b * block, n * block)

    def near_head(h, carry):
        vt = jnp.transpose(v_buf[h])
        last_vt[h] = vt[:, rows - block :]
        for b in range(blocks):
            q = q_buf[h, span_of(b), :]
            scores = dot_t(k_buf[h, span_of(b), :], q)
            if b:
                scores = jnp.where(here, scores, dot_t(k_buf[h, span_of(b - 1), :], q))
            else:
                scores = jnp.where(here, scores, NEG)
            top = jnp.max(scores, axis=0, keepdims=True)
            weights = jnp.exp2((scores - top) * gain)
            total = jnp.sum(weights, axis=0, keepdims=True)
            now = jnp.where(here, weights, 0.0).astype(BF16)
            if b:
                before = jnp.where(here, 0.0, weights).astype(BF16)
                both = jnp.concatenate([before, now], axis=0)
                acc = dot(vt[:, (b - 1) * block : (b + 1) * block], both)
            else:
                acc = dot(vt[:, :block], now)
            top_s[h, :, span_of(b)] = top
            total_s[h, :, span_of(b)] = total
            acc_s[h, :, span_of(b)] = acc
        return carry

    def respond(first, last):
        @pl.when(has_next)
        def _():
            for h in range(first, last):
                ask(h, spot).wait_recv()
                scores = jnp.where(here, NEG, dot_t(k_buf[h, span_of(blocks - 1), :], asked[h]))
                top = jnp.max(scores, axis=0, keepdims=True)
                weights = jnp.where(here, 0.0, jnp.exp2((scores - top) * gain))
                stat[h] = jnp.concatenate([top, jnp.sum(weights, axis=0, keepdims=True)], axis=0)
                answer[h] = dot(last_vt[h], weights.astype(BF16)).astype(BF16)
                give(h, spot + 1).start()
                give_stat(h, spot + 1).start()

    def relay(source):
        for g in range(chunks):
            sum_copy(source, g, spot).wait_recv()

            @pl.when(has_next)
            def _():
                sum_copy(source, g, spot + 1).start()

    def relay_if(distance):
        @pl.when(spot >= distance)
        def _():
            relay(spot - distance)

    marks = [min(heads, n) for n in (1, 3, heads)]
    lax.fori_loop(0, marks[0], near_head, 0)
    respond(0, marks[0])
    lax.fori_loop(marks[0], marks[1], near_head, 0)
    relay_if(1)
    respond(marks[0], marks[1])
    lax.fori_loop(marks[1], marks[2], near_head, 0)
    relay_if(2)
    respond(marks[1], marks[2])

    def relay_rest(d, c):
        relay(spot - d)
        return c

    lax.fori_loop(3, spot + 1, relay_rest, 0)

    def far_chunk(h, j, top, total, acc):
        keys, values = (
            jnp.concatenate([summ[j * per + i, h, w] for i in range(per)], axis=0)
            for w in range(2)
        )
        scores = dot_t(keys, q_buf[h])
        limit = [(spot * blocks + b) * sums - j * block for b in range(blocks)]
        scores = jnp.concatenate(
            [
                jnp.where(key_at < limit[b], scores[:, b * block : (b + 1) * block], NEG)
                for b in range(blocks)
            ],
            axis=1,
        )
        old, top = top, jnp.maximum(top, jnp.max(scores, axis=0, keepdims=True))
        weights = jnp.exp2((scores - top) * gain)
        fade = jnp.exp2((old - top) * gain)
        total = total * fade + jnp.sum(weights, axis=0, keepdims=True)
        return top, total, acc * fade + dot(jnp.transpose(values), weights.astype(BF16))

    def far_head(h, carry):
        if slots == per:
            top, total, acc = far_chunk(h, 0, top_s[h], total_s[h], acc_s[h])
        else:
            def chunk(j, c):
                top_s[h], total_s[h], acc_s[h] = far_chunk(h, j, top_s[h], total_s[h], acc_s[h])
                return c

            lax.fori_loop(0, (spot * own + own - sums + block - 1) // block, chunk, 0)
            top, total, acc = top_s[h], total_s[h], acc_s[h]
        top_s[h, :, :block] = top[:, :block]
        total_s[h, :, :block] = total[:, :block]
        acc_s[h, :, :block] = acc[:, :block]
        out = (acc[:, block:] * (1.0 / total[:, block:])).astype(BF16)
        o_ref[h, block:, :] = jnp.transpose(out)
        return carry

    lax.fori_loop(0, heads, far_head, 0)

    def merge(h, carry):
        @pl.when(has_prev)
        def _():
            give(h, spot).wait_recv()
            give_stat(h, spot).wait_recv()

        old, new = top_s[h, :, :block], stat_back[h, 0:1, :]
        top = jnp.maximum(old, new)
        fade, new_fade = jnp.exp2((old - top) * gain), jnp.exp2((new - top) * gain)
        total = total_s[h, :, :block] * fade + stat_back[h, 1:2, :] * new_fade
        acc = acc_s[h, :, :block] * fade + back[h].astype(F32) * new_fade
        o_ref[h, :block, :] = jnp.transpose((acc * (1.0 / total)).astype(BF16))
        return carry

    lax.fori_loop(0, heads, merge, 0)

    @pl.when(has_prev)
    def _():
        for h in range(heads):
            ask(h, spot - 1).wait_send()

    @pl.when(has_next)
    def _():
        for h in range(heads):
            give(h, spot + 1).wait_send()
            give_stat(h, spot + 1).wait_send()

        def sent(i, c):
            for g in range(chunks):
                sum_copy(i, g, spot + 1).wait_send()
            return c

        lax.fori_loop(0, spot + 1, sent, 0)


def on_device(peers, queries, keys, values, pool_keys, pool_values):
    rows, heads, width = queries.shape
    sums, block = pool_keys.shape[1], pool_keys.shape[2]
    own = rows // block * sums
    per = block // own
    slots = -(-peers // per) * per
    span = 2 if heads % 2 == 0 else 1
    q, k, v = (jnp.moveaxis(x, 1, 0) for x in (queries, keys, values))
    hbm = pl.BlockSpec(memory_space=pltpu.HBM)
    out = pl.pallas_call(
        functools.partial(kernel, peers, span),
        out_shape=pltpu.VMEM((heads, rows, width), BF16),
        in_specs=[hbm] * 5,
        out_specs=pl.BlockSpec(memory_space=pltpu.VMEM),
        scratch_shapes=[
            pltpu.VMEM((heads, rows, width), BF16),
            pltpu.VMEM((heads, rows, width), BF16),
            pltpu.VMEM((heads, rows, width), BF16),
            pltpu.VMEM(pool_keys.shape, BF16),
            pltpu.VMEM(pool_values.shape, BF16),
            pltpu.VMEM((heads, width, block), BF16),
            pltpu.VMEM((heads, block, width), BF16),
            pltpu.VMEM((heads, width, block), BF16),
            pltpu.VMEM((heads, width, block), BF16),
            pltpu.VMEM((heads, 2, block), F32),
            pltpu.VMEM((heads, 2, block), F32),
            pltpu.VMEM((slots, heads, 2, own, width), BF16),
            pltpu.VMEM((heads, 1, rows), F32),
            pltpu.VMEM((heads, 1, rows), F32),
            pltpu.VMEM((heads, width, rows), F32),
            pltpu.SemaphoreType.DMA((3, heads)),
            pltpu.SemaphoreType.DMA((2,)),
            pltpu.SemaphoreType.DMA((heads,)),
            pltpu.SemaphoreType.DMA((heads,)),
            pltpu.SemaphoreType.DMA((heads,)),
            pltpu.SemaphoreType.DMA((heads,)),
            pltpu.SemaphoreType.DMA((2, heads)),
            pltpu.SemaphoreType.DMA((slots, heads // span)),
            pltpu.SemaphoreType.DMA((slots, heads // span)),
        ],
        compiler_params=pltpu.CompilerParams(
            collective_id=0, has_side_effects=True, vmem_limit_bytes=40 * 1024 * 1024
        ),
    )(*(pltpu.with_memory_space_constraint(x, pltpu.HBM) for x in (q, k, v, pool_keys, pool_values)))
    return jnp.moveaxis(out, 0, 1)


def solution(mesh):
    in_specs = (
        P(("groups", "seq"), "heads", None),
        P(("groups", "seq"), "heads", None),
        P(("groups", "seq"), "heads", None),
        P("heads", None, None),
        P("heads", None, None),
    )
    out_specs = P(("groups", "seq"), "heads", None)
    return jax.shard_map(
        functools.partial(on_device, mesh.shape["seq"]),
        mesh=mesh, in_specs=in_specs, out_specs=out_specs, check_vma=False,
    )
```

```python
import functools
import math

import jax
import jax.numpy as jnp
from jax import lax
from jax.experimental import pallas as pl
from jax.experimental.pallas import tpu as pltpu
from jax.sharding import PartitionSpec as P

NEG = -1e30
F32 = jnp.float32
BF16 = jnp.bfloat16


def dot_t(a, b):
    return lax.dot_general(a, b, (((1,), (1,)), ((), ())), preferred_element_type=F32)


def dot(a, b):
    return jnp.dot(a, b, preferred_element_type=F32)


def kernel(
    peers, span, q_hbm, k_hbm, v_hbm, pk_hbm, pv_hbm, o_ref,
    q_buf, k_buf, v_buf, pk_ref, pv_ref, last_vt, asked, answer, back, stat, stat_back,
    summ, top_s, total_s, fade_s, acc_s, far_w,
    in_sem, pool_sem, ask_send, ask_recv, back_send, back_recv, stat_sem, sum_send, sum_recv,
):
    heads, rows, width = q_buf.shape
    sums, block = pk_ref.shape[1], pk_ref.shape[2]
    blocks = rows // block
    own = blocks * sums
    per = block // own
    slots = summ.shape[0]
    chunks = heads // span
    gain = (width ** -0.5) * math.log2(math.e)
    spot = lax.axis_index("seq")
    has_next = spot < peers - 1
    has_prev = spot > 0

    pools = [
        pltpu.make_async_copy(src, dst, pool_sem.at[i])
        for i, (src, dst) in enumerate(((pk_hbm, pk_ref), (pv_hbm, pv_ref)))
    ]
    for copy in pools:
        copy.start()

    def load(i, h):
        src, dst = ((k_hbm, k_buf), (v_hbm, v_buf), (q_hbm, q_buf))[i]
        return pltpu.make_async_copy(src.at[h], dst.at[h], in_sem.at[i, h])

    for h in range(heads):
        load(0, h).start()
        load(1, h).start()
    for h in range(heads):
        load(2, h).start()

    barrier = pltpu.get_barrier_semaphore()

    def greet(to):
        pl.semaphore_signal(
            barrier, inc=1, device_id={"seq": to}, device_id_type=pl.DeviceIdType.MESH
        )

    @pl.when(has_prev)
    def _():
        greet(spot - 1)

    @pl.when(has_next)
    def _():
        greet(spot + 1)

    def clear(i, c):
        summ[i] = jnp.zeros(summ.shape[1:], BF16)
        return c

    lax.fori_loop(spot + 1, slots, clear, 0)

    @pl.when(spot == 0)
    def _():
        back[...] = jnp.zeros(back.shape, BF16)
        top_row = lax.broadcasted_iota(jnp.int32, stat_back.shape, 1) == 0
        stat_back[...] = jnp.where(top_row, NEG, 0.0)

    pl.semaphore_wait(barrier, jnp.where(has_prev, 1, 0) + jnp.where(has_next, 1, 0))

    def remote(src, dst, send_sem, recv_sem, to):
        return pltpu.make_async_remote_copy(
            src_ref=src,
            dst_ref=dst,
            send_sem=send_sem,
            recv_sem=recv_sem,
            device_id={"seq": to},
            device_id_type=pl.DeviceIdType.MESH,
        )

    def ask(h, to):
        src = q_hbm.at[h, pl.ds(0, block), :]
        return remote(src, asked.at[h], ask_send.at[h], ask_recv.at[h], to)

    def give(h, to):
        return remote(answer.at[h], back.at[h], back_send.at[h], back_recv.at[h], to)

    def give_stat(h, to):
        return remote(stat.at[h], stat_back.at[h], stat_sem.at[0, h], stat_sem.at[1, h], to)

    def sum_copy(source, g, to):
        at = summ.at[source, pl.ds(g * span, span)]
        return remote(at, at, sum_send.at[source, g], sum_recv.at[source, g], to)

    @pl.when(has_prev)
    def _():
        for h in range(heads):
            ask(h, spot - 1).start()

    def region(body):
        pl.when(spot >= 0)(body)

    def heads_of(g):
        return [g * span + i for i in range(span)]

    def span_of(b, n=1):
        return pl.ds(b * block, n * block)

    for copy in pools:
        copy.wait()
    for g in range(chunks):
        for h in heads_of(g):
            load(0, h).wait()
            load(1, h).wait()
        for h in heads_of(g):
            for which, (pool, buf) in enumerate(((pk_ref, k_buf), (pv_ref, v_buf))):
                parts = [dot(pool[h], buf[h, span_of(b), :]) for b in range(blocks)]
                summ[spot, h, which] = jnp.concatenate(parts, axis=0).astype(BF16)

        @pl.when(has_next)
        def _():
            sum_copy(spot, g, spot + 1).start()

    key_at = lax.broadcasted_iota(jnp.int32, (block, block), 0)
    query_at = lax.broadcasted_iota(jnp.int32, (block, block), 1)
    here = key_at <= query_at

    def soften(scores):
        top = jnp.max(scores, axis=0, keepdims=True)
        return top, jnp.exp2((scores - top) * gain)

    def near(g):
        @region
        def _():
            for h in heads_of(g):
                for b in range(blocks):
                    q = q_buf[h, span_of(b), :]
                    if b:
                        scores = dot_t(k_buf[h, span_of(b - 1, 2), :], q)
                        scores = jnp.where(here, scores[block:], scores[:block])
                    else:
                        scores = jnp.where(here, dot_t(k_buf[h, span_of(b), :], q), NEG)
                    top, weights = soften(scores)
                    top_s[h, :, span_of(b)] = top
                    total_s[h, :, span_of(b)] = jnp.sum(weights, axis=0, keepdims=True)
                    acc_s[h, :, span_of(b)] = weights

        @region
        def _():
            for h in heads_of(g):
                vt = jnp.transpose(v_buf[h])
                last_vt[h] = vt[:, rows - block :]
                for b in range(blocks):
                    weights = acc_s[h, :, span_of(b)]
                    both = jnp.where(here, weights, 0.0).astype(BF16)
                    if b:
                        before = jnp.where(here, 0.0, weights).astype(BF16)
                        both = jnp.concatenate([before, both], axis=0)
                    acc_s[h, :, span_of(b)] = dot(vt[:, max(b - 1, 0) * block : (b + 1) * block], both)

    def respond(g):
        @pl.when(has_next)
        def _():
            for h in heads_of(g):
                ask(h, spot).wait_recv()
            scores = [dot_t(k_buf[h, span_of(blocks - 1), :], asked[h]) for h in heads_of(g)]
            for h, s in zip(heads_of(g), scores):
                top, weights = soften(jnp.where(here, NEG, s))
                weights = jnp.where(here, 0.0, weights)
                stat[h] = jnp.concatenate([top, jnp.sum(weights, axis=0, keepdims=True)], axis=0)
                answer[h] = dot(last_vt[h], weights.astype(BF16)).astype(BF16)
            for h in heads_of(g):
                give(h, spot + 1).start()
                give_stat(h, spot + 1).start()

    def relay(source):
        for g in range(chunks):
            sum_copy(source, g, spot).wait_recv()

            @pl.when(has_next)
            def _():
                sum_copy(source, g, spot + 1).start()

    def relay_if(distance):
        @pl.when(spot >= distance)
        def _():
            relay(spot - distance)

    def relay_rest(d, c):
        relay(spot - d)
        return c

    def far_weights(g, j):
        @region
        def _():
            for h in heads_of(g):
                keys = jnp.concatenate([summ[j * per + i, h, 0] for i in range(per)], axis=0)
                scores = dot_t(keys, q_buf[h])
                for b in range(blocks):
                    limit = (spot * blocks + b) * sums - j * block
                    part = jnp.where(key_at < limit, scores[:, b * block : (b + 1) * block], NEG)
                    old = top_s[h, :, span_of(b)]
                    top = jnp.maximum(old, jnp.max(part, axis=0, keepdims=True))
                    weights = jnp.exp2((part - top) * gain)
                    fade = jnp.exp2((old - top) * gain)
                    top_s[h, :, span_of(b)] = top
                    fade_s[h, :, span_of(b)] = fade
                    total = total_s[h, :, span_of(b)]
                    total_s[h, :, span_of(b)] = total * fade + jnp.sum(weights, axis=0, keepdims=True)
                    far_w[h, :, span_of(b)] = weights.astype(BF16)

    def far_values(g, j, finish):
        @region
        def _():
            for h in heads_of(g):
                values = jnp.concatenate([summ[j * per + i, h, 1] for i in range(per)], axis=0)
                acc = acc_s[h] * fade_s[h] + dot(jnp.transpose(values), far_w[h])
                if finish:
                    acc_s[h, :, :block] = acc[:, :block]
                    write(h, acc)
                else:
                    acc_s[h] = acc

    def write(h, acc):
        out = acc[:, block:] * (1.0 / total_s[h, :, block:])
        o_ref[h, block:, :] = jnp.transpose(out.astype(BF16))

    def far(g):
        if slots == per:
            far_weights(g, 0)
            far_values(g, 0, True)
            return

        def chunk(j, c):
            far_weights(g, j)
            far_values(g, j, False)
            return c

        lax.fori_loop(0, (spot * own + own - sums + block - 1) // block, chunk, 0)

        @region
        def _():
            for h in heads_of(g):
                write(h, acc_s[h])

    def merge(g):
        @pl.when(has_prev)
        def _():
            for h in heads_of(g):
                give(h, spot).wait_recv()
                give_stat(h, spot).wait_recv()

        @region
        def _():
            for h in heads_of(g):
                old, new = top_s[h, :, :block], stat_back[h, 0:1, :]
                top = jnp.maximum(old, new)
                fade, new_fade = jnp.exp2((old - top) * gain), jnp.exp2((new - top) * gain)
                total = total_s[h, :, :block] * fade + stat_back[h, 1:2, :] * new_fade
                acc = acc_s[h, :, :block] * fade + back[h].astype(F32) * new_fade
                o_ref[h, :block, :] = jnp.transpose((acc * (1.0 / total)).astype(BF16))

    for h in range(heads):
        load(2, h).wait()
    near(0)
    relay_if(1)
    for g in range(1, chunks):
        near(g)
    respond(0)
    relay_if(2)
    for g in range(1, chunks):
        respond(g)
    lax.fori_loop(3, spot + 1, relay_rest, 0)
    for g in range(chunks):
        far(g)
    for g in range(chunks):
        merge(g)

    @pl.when(has_prev)
    def _():
        for h in range(heads):
            ask(h, spot - 1).wait_send()

    @pl.when(has_next)
    def _():
        for h in range(heads):
            give(h, spot + 1).wait_send()
            give_stat(h, spot + 1).wait_send()

        def sent(i, c):
            for g in range(chunks):
                sum_copy(i, g, spot + 1).wait_send()
            return c

        lax.fori_loop(0, spot + 1, sent, 0)


def on_device(peers, queries, keys, values, pool_keys, pool_values):
    rows, heads, width = queries.shape
    sums, block = pool_keys.shape[1], pool_keys.shape[2]
    own = rows // block * sums
    per = block // own
    slots = -(-peers // per) * per
    span = next(n for n in (3, 2, 1) if heads % n == 0)
    q, k, v = (jnp.moveaxis(x, 1, 0) for x in (queries, keys, values))
    hbm = pl.BlockSpec(memory_space=pltpu.HBM)
    out = pl.pallas_call(
        functools.partial(kernel, peers, span),
        out_shape=pltpu.VMEM((heads, rows, width), BF16),
        in_specs=[hbm] * 5,
        out_specs=pl.BlockSpec(memory_space=pltpu.VMEM),
        scratch_shapes=[
            pltpu.VMEM((heads, rows, width), BF16),
            pltpu.VMEM((heads, rows, width), BF16),
            pltpu.VMEM((heads, rows, width), BF16),
            pltpu.VMEM(pool_keys.shape, BF16),
            pltpu.VMEM(pool_values.shape, BF16),
            pltpu.VMEM((heads, width, block), BF16),
            pltpu.VMEM((heads, block, width), BF16),
            pltpu.VMEM((heads, width, block), BF16),
            pltpu.VMEM((heads, width, block), BF16),
            pltpu.VMEM((heads, 2, block), F32),
            pltpu.VMEM((heads, 2, block), F32),
            pltpu.VMEM((slots, heads, 2, own, width), BF16),
            pltpu.VMEM((heads, 1, rows), F32),
            pltpu.VMEM((heads, 1, rows), F32),
            pltpu.VMEM((heads, 1, rows), F32),
            pltpu.VMEM((heads, width, rows), F32),
            pltpu.VMEM((heads, block, rows), BF16),
            pltpu.SemaphoreType.DMA((3, heads)),
            pltpu.SemaphoreType.DMA((2,)),
            pltpu.SemaphoreType.DMA((heads,)),
            pltpu.SemaphoreType.DMA((heads,)),
            pltpu.SemaphoreType.DMA((heads,)),
            pltpu.SemaphoreType.DMA((heads,)),
            pltpu.SemaphoreType.DMA((2, heads)),
            pltpu.SemaphoreType.DMA((slots, heads // span)),
            pltpu.SemaphoreType.DMA((slots, heads // span)),
        ],
        compiler_params=pltpu.CompilerParams(
            collective_id=0, has_side_effects=True, vmem_limit_bytes=40 * 1024 * 1024
        ),
    )(*(pltpu.with_memory_space_constraint(x, pltpu.HBM) for x in (q, k, v, pool_keys, pool_values)))
    return jnp.moveaxis(out, 0, 1)


def solution(mesh):
    in_specs = (
        P(("groups", "seq"), "heads", None),
        P(("groups", "seq"), "heads", None),
        P(("groups", "seq"), "heads", None),
        P("heads", None, None),
        P("heads", None, None),
    )
    out_specs = P(("groups", "seq"), "heads", None)
    return jax.shard_map(
        functools.partial(on_device, mesh.shape["seq"]),
        mesh=mesh, in_specs=in_specs, out_specs=out_specs, check_vma=False,
    )
```

```python
import functools
import math

import jax
import jax.numpy as jnp
from jax import lax
from jax.experimental import pallas as pl
from jax.experimental.pallas import tpu as pltpu
from jax.sharding import PartitionSpec as P

NEG = -1e30
F32 = jnp.float32
BF16 = jnp.bfloat16


def dot_t(a, b):
    return lax.dot_general(a, b, (((1,), (1,)), ((), ())), preferred_element_type=F32)


def dot(a, b):
    return jnp.dot(a, b, preferred_element_type=F32)


def kernel(
    peers, span, step, q_hbm, k_hbm, v_hbm, pk_hbm, pv_hbm, o_ref,
    q_buf, k_buf, v_buf, pk_ref, pv_ref, last_vt, asked, answer, back, stat, stat_back,
    summ, top_s, total_s, fade_s, acc_s, far_w,
    in_sem, pool_sem, ask_send, ask_recv, back_send, back_recv, stat_sem, sum_send, sum_recv, skip_send,
):
    heads, rows, width = q_buf.shape
    sums, block = pk_ref.shape[1], pk_ref.shape[2]
    blocks = rows // block
    own = blocks * sums
    per = block // own
    slots = summ.shape[0]
    chunks = heads // span
    gain = (width ** -0.5) * math.log2(math.e)
    spot = lax.axis_index("seq")
    has_next = spot < peers - 1
    has_prev = spot > 0
    even = lax.rem(spot, 2) == 0
    has_skip = jnp.logical_and(even, spot < peers - 2)
    from_skip = jnp.logical_and(even, spot > 1)

    barrier = pltpu.get_barrier_semaphore()

    def greet(to):
        pl.semaphore_signal(
            barrier, inc=1, device_id={"seq": to}, device_id_type=pl.DeviceIdType.MESH
        )

    @pl.when(has_prev)
    def _():
        greet(spot - 1)

    @pl.when(has_next)
    def _():
        greet(spot + 1)

    @pl.when(from_skip)
    def _():
        greet(spot - 2)

    pools = [
        pltpu.make_async_copy(src, dst, pool_sem.at[i])
        for i, (src, dst) in enumerate(((pk_hbm, pk_ref), (pv_hbm, pv_ref)))
    ]
    for copy in pools:
        copy.start()

    def load(i, h):
        src, dst = ((k_hbm, k_buf), (v_hbm, v_buf), (q_hbm, q_buf))[i]
        return pltpu.make_async_copy(src.at[h], dst.at[h], in_sem.at[i, h])

    for h in range(heads):
        load(0, h).start()
        load(1, h).start()
    for h in range(heads):
        load(2, h).start()

    def remote(src, dst, send_sem, recv_sem, to):
        return pltpu.make_async_remote_copy(
            src_ref=src,
            dst_ref=dst,
            send_sem=send_sem,
            recv_sem=recv_sem,
            device_id={"seq": to},
            device_id_type=pl.DeviceIdType.MESH,
        )

    def group(g):
        return pl.ds(g * span, span)

    def ask(g, to):
        src = q_hbm.at[group(g), pl.ds(0, block), :]
        return remote(src, asked.at[group(g)], ask_send.at[g], ask_recv.at[g], to)

    def give(g, to):
        src, dst = answer.at[group(g)], back.at[group(g)]
        return remote(src, dst, back_send.at[g], back_recv.at[g], to)

    def give_stat(g, to):
        src, dst = stat.at[group(g)], stat_back.at[group(g)]
        return remote(src, dst, stat_sem.at[0, g], stat_sem.at[1, g], to)

    def sum_copy(source, p, to):
        at = summ.at[source, pl.ds(p * step, step)]
        return remote(at, at, sum_send.at[source, p], sum_recv.at[source, p], to)

    def skip_copy(p):
        at = summ.at[spot, pl.ds(p * step, step)]
        return remote(at, at, skip_send.at[p], sum_recv.at[spot, p], spot + 2)

    def enter():
        known = (has_prev, has_next, has_skip)
        pl.semaphore_wait(barrier, sum(jnp.where(one, 1, 0) for one in known))

    def send_asks():
        @pl.when(has_prev)
        def _():
            for g in range(chunks):
                ask(g, spot - 1).start()

    def region(body):
        pl.when(spot >= 0)(body)

    def heads_of(g):
        return [g * span + i for i in range(span)]

    def parts_of(g):
        return range(g * span // step, (g + 1) * span // step)

    def span_of(b, n=1):
        return pl.ds(b * block, n * block)

    @pl.when(jnp.logical_not(has_next))
    def _():
        enter()
        send_asks()

    for copy in pools:
        copy.wait()
    for g in range(chunks):
        for h in heads_of(g):
            load(0, h).wait()
            load(1, h).wait()
        for h in heads_of(g):
            for which, (pool, buf) in enumerate(((pk_ref, k_buf), (pv_ref, v_buf))):
                parts = [dot(pool[h], buf[h, span_of(b), :]) for b in range(blocks)]
                summ[spot, h, which] = jnp.concatenate(parts, axis=0).astype(BF16)

        @pl.when(has_next)
        def _():
            if g == 0:
                enter()
            for p in parts_of(g):
                sum_copy(spot, p, spot + 1).start()

            @pl.when(has_skip)
            def _():
                for p in parts_of(g):
                    skip_copy(p).start()

            if g == 0:
                send_asks()

    def clear(i, c):
        summ[i] = jnp.zeros(summ.shape[1:], BF16)
        return c

    lax.fori_loop(spot + 1, slots, clear, 0)

    @pl.when(spot == 0)
    def _():
        back[...] = jnp.zeros(back.shape, BF16)
        top_row = lax.broadcasted_iota(jnp.int32, stat_back.shape, 1) == 0
        stat_back[...] = jnp.where(top_row, NEG, 0.0)

    key_at = lax.broadcasted_iota(jnp.int32, (block, block), 0)
    query_at = lax.broadcasted_iota(jnp.int32, (block, block), 1)
    here = key_at <= query_at

    def soften(scores):
        top = jnp.max(scores, axis=0, keepdims=True)
        return top, jnp.exp2((scores - top) * gain)

    def near(g):
        @region
        def _():
            for h in heads_of(g):
                for b in range(blocks):
                    q = q_buf[h, span_of(b), :]
                    if b:
                        scores = dot_t(k_buf[h, span_of(b - 1, 2), :], q)
                        scores = jnp.where(here, scores[block:], scores[:block])
                    else:
                        scores = jnp.where(here, dot_t(k_buf[h, span_of(b), :], q), NEG)
                    top, weights = soften(scores)
                    top_s[h, :, span_of(b)] = top
                    total_s[h, :, span_of(b)] = jnp.sum(weights, axis=0, keepdims=True)
                    acc_s[h, :, span_of(b)] = weights

        @region
        def _():
            for h in heads_of(g):
                vt = jnp.transpose(v_buf[h])
                last_vt[h] = vt[:, rows - block :]
                for b in range(blocks):
                    weights = acc_s[h, :, span_of(b)]
                    both = jnp.where(here, weights, 0.0).astype(BF16)
                    if b:
                        before = jnp.where(here, 0.0, weights).astype(BF16)
                        both = jnp.concatenate([before, both], axis=0)
                    acc_s[h, :, span_of(b)] = dot(vt[:, max(b - 1, 0) * block : (b + 1) * block], both)

    def respond(g):
        @pl.when(has_next)
        def _():
            ask(g, spot).wait_recv()
            scores = [dot_t(k_buf[h, span_of(blocks - 1), :], asked[h]) for h in heads_of(g)]
            for h, s in zip(heads_of(g), scores):
                top, weights = soften(jnp.where(here, NEG, s))
                weights = jnp.where(here, 0.0, weights)
                stat[h] = jnp.concatenate([top, jnp.sum(weights, axis=0, keepdims=True)], axis=0)
                answer[h] = dot(last_vt[h], weights.astype(BF16)).astype(BF16)
            give(g, spot + 1).start()
            give_stat(g, spot + 1).start()

    def forwards(d):
        first = jnp.logical_or(even, d != 1)
        return jnp.logical_and(has_next, jnp.logical_and(spot >= d, first))

    def relay(g, d):
        @pl.when(forwards(d))
        def _():
            for p in parts_of(g):
                sum_copy(spot - d, p, spot).wait_recv()
                sum_copy(spot - d, p, spot + 1).start()

    def relay_rest(d, c):
        for g in range(chunks):
            relay(g, d)
        return c

    def land(g):
        def one(d, c):
            @pl.when(jnp.logical_not(forwards(d)))
            def _():
                for p in parts_of(g):
                    sum_copy(spot - d, p, spot).wait_recv()

            return c

        lax.fori_loop(1, spot + 1, one, 0)

    def far_weights(g, j):
        @region
        def _():
            for h in heads_of(g):
                keys = jnp.concatenate([summ[j * per + i, h, 0] for i in range(per)], axis=0)
                scores = dot_t(keys, q_buf[h])
                for b in range(blocks):
                    limit = (spot * blocks + b) * sums - j * block
                    part = jnp.where(key_at < limit, scores[:, b * block : (b + 1) * block], NEG)
                    old = top_s[h, :, span_of(b)]
                    top = jnp.maximum(old, jnp.max(part, axis=0, keepdims=True))
                    weights = jnp.exp2((part - top) * gain)
                    fade = jnp.exp2((old - top) * gain)
                    top_s[h, :, span_of(b)] = top
                    fade_s[h, :, span_of(b)] = fade
                    total = total_s[h, :, span_of(b)]
                    total_s[h, :, span_of(b)] = total * fade + jnp.sum(weights, axis=0, keepdims=True)
                    far_w[h, :, span_of(b)] = weights.astype(BF16)

    def far_values(g, j, finish):
        @region
        def _():
            for h in heads_of(g):
                values = jnp.concatenate([summ[j * per + i, h, 1] for i in range(per)], axis=0)
                acc = acc_s[h] * fade_s[h] + dot(jnp.transpose(values), far_w[h])
                if finish:
                    acc_s[h, :, :block] = acc[:, :block]
                    write(h, acc)
                else:
                    acc_s[h] = acc

    def write(h, acc):
        out = acc[:, block:] * (1.0 / total_s[h, :, block:])
        o_ref[h, block:, :] = jnp.transpose(out.astype(BF16))

    def far(g):
        if slots == per:
            far_weights(g, 0)
            far_values(g, 0, True)
            return

        def chunk(j, c):
            far_weights(g, j)
            far_values(g, j, False)
            return c

        lax.fori_loop(0, (spot * own + own - sums + block - 1) // block, chunk, 0)

        @region
        def _():
            for h in heads_of(g):
                write(h, acc_s[h])

    def merge(g):
        @pl.when(has_prev)
        def _():
            give(g, spot).wait_recv()
            give_stat(g, spot).wait_recv()

        @region
        def _():
            for h in heads_of(g):
                old, new = top_s[h, :, :block], stat_back[h, 0:1, :]
                top = jnp.maximum(old, new)
                fade, new_fade = jnp.exp2((old - top) * gain), jnp.exp2((new - top) * gain)
                total = total_s[h, :, :block] * fade + stat_back[h, 1:2, :] * new_fade
                acc = acc_s[h, :, :block] * fade + back[h].astype(F32) * new_fade
                o_ref[h, :block, :] = jnp.transpose((acc * (1.0 / total)).astype(BF16))

    for h in range(heads):
        load(2, h).wait()
    for g in range(chunks):
        near(g)
    for g in range(chunks):
        relay(g, 1)
        relay(g, 2)
        respond(g)
    lax.fori_loop(3, spot + 1, relay_rest, 0)
    for g in range(chunks):
        land(g)
        far(g)
    for g in range(chunks):
        merge(g)

    @pl.when(has_prev)
    def _():
        for g in range(chunks):
            ask(g, spot - 1).wait_send()

    @pl.when(has_next)
    def _():
        for g in range(chunks):
            give(g, spot + 1).wait_send()
            give_stat(g, spot + 1).wait_send()

        for p in range(heads // step):
            sum_copy(spot, p, spot + 1).wait_send()

        @pl.when(has_skip)
        def _():
            for p in range(heads // step):
                skip_copy(p).wait_send()

        def sent(d, c):
            @pl.when(forwards(d))
            def _():
                for p in range(heads // step):
                    sum_copy(spot - d, p, spot + 1).wait_send()

            return c

        lax.fori_loop(1, spot + 1, sent, 0)


def on_device(peers, queries, keys, values, pool_keys, pool_values):
    rows, heads, width = queries.shape
    sums, block = pool_keys.shape[1], pool_keys.shape[2]
    own = rows // block * sums
    per = block // own
    slots = -(-peers // per) * per
    span = next(n for n in (3, 2, 1) if heads % n == 0)
    step = span
    chunks = heads // span
    q, k, v = (jnp.moveaxis(x, 1, 0) for x in (queries, keys, values))
    hbm = pl.BlockSpec(memory_space=pltpu.HBM)
    out = pl.pallas_call(
        functools.partial(kernel, peers, span, step),
        out_shape=pltpu.VMEM((heads, rows, width), BF16),
        in_specs=[hbm] * 5,
        out_specs=pl.BlockSpec(memory_space=pltpu.VMEM),
        scratch_shapes=[
            pltpu.VMEM((heads, rows, width), BF16),
            pltpu.VMEM((heads, rows, width), BF16),
            pltpu.VMEM((heads, rows, width), BF16),
            pltpu.VMEM(pool_keys.shape, BF16),
            pltpu.VMEM(pool_values.shape, BF16),
            pltpu.VMEM((heads, width, block), BF16),
            pltpu.VMEM((heads, block, width), BF16),
            pltpu.VMEM((heads, width, block), BF16),
            pltpu.VMEM((heads, width, block), BF16),
            pltpu.VMEM((heads, 2, block), F32),
            pltpu.VMEM((heads, 2, block), F32),
            pltpu.VMEM((slots, heads, 2, own, width), BF16),
            pltpu.VMEM((heads, 1, rows), F32),
            pltpu.VMEM((heads, 1, rows), F32),
            pltpu.VMEM((heads, 1, rows), F32),
            pltpu.VMEM((heads, width, rows), F32),
            pltpu.VMEM((heads, block, rows), BF16),
            pltpu.SemaphoreType.DMA((3, heads)),
            pltpu.SemaphoreType.DMA((2,)),
            pltpu.SemaphoreType.DMA((chunks,)),
            pltpu.SemaphoreType.DMA((chunks,)),
            pltpu.SemaphoreType.DMA((chunks,)),
            pltpu.SemaphoreType.DMA((chunks,)),
            pltpu.SemaphoreType.DMA((2, chunks)),
            pltpu.SemaphoreType.DMA((slots, heads // step)),
            pltpu.SemaphoreType.DMA((slots, heads // step)),
            pltpu.SemaphoreType.DMA((heads // step,)),
        ],
        compiler_params=pltpu.CompilerParams(
            collective_id=0, has_side_effects=True, vmem_limit_bytes=40 * 1024 * 1024
        ),
    )(*(pltpu.with_memory_space_constraint(x, pltpu.HBM) for x in (q, k, v, pool_keys, pool_values)))
    return jnp.moveaxis(out, 0, 1)


def solution(mesh):
    in_specs = (
        P(("groups", "seq"), "heads", None),
        P(("groups", "seq"), "heads", None),
        P(("groups", "seq"), "heads", None),
        P("heads", None, None),
        P("heads", None, None),
    )
    out_specs = P(("groups", "seq"), "heads", None)
    return jax.shard_map(
        functools.partial(on_device, mesh.shape["seq"]),
        mesh=mesh, in_specs=in_specs, out_specs=out_specs, check_vma=False,
    )
```

```python
import functools
import math

import jax
import jax.numpy as jnp
from jax import lax
from jax.experimental import pallas as pl
from jax.experimental.pallas import tpu as pltpu
from jax.sharding import PartitionSpec as P

NEG = -1e30
F32 = jnp.float32
BF16 = jnp.bfloat16


def dot_t(a, b):
    return lax.dot_general(a, b, (((1,), (1,)), ((), ())), preferred_element_type=F32)


def dot(a, b):
    return jnp.dot(a, b, preferred_element_type=F32)


def kernel(
    peers, span, step, q_hbm, k_hbm, v_hbm, pk_hbm, pv_hbm, o_ref,
    q_buf, k_buf, v_buf, pk_ref, pv_ref, last_vt, asked, answer, back, stat, stat_back,
    summ, top_s, total_s, fade_s, acc_s, far_w,
    in_sem, pool_sem, ask_send, ask_recv, back_send, back_recv, stat_sem, sum_send, sum_recv, skip_send,
):
    heads, rows, width = q_buf.shape
    sums, block = pk_ref.shape[1], pk_ref.shape[2]
    blocks = rows // block
    own = blocks * sums
    per = block // own
    slots = summ.shape[0]
    chunks = heads // span
    gain = (width ** -0.5) * math.log2(math.e)
    spot = lax.axis_index("seq")
    has_next = spot < peers - 1
    has_prev = spot > 0
    even = lax.rem(spot, 2) == 0
    has_skip = jnp.logical_and(even, spot < peers - 2)
    from_skip = jnp.logical_and(even, spot > 1)

    barrier = pltpu.get_barrier_semaphore()

    def greet(to):
        pl.semaphore_signal(
            barrier, inc=1, device_id={"seq": to}, device_id_type=pl.DeviceIdType.MESH
        )

    @pl.when(has_prev)
    def _():
        greet(spot - 1)

    @pl.when(has_next)
    def _():
        greet(spot + 1)

    @pl.when(from_skip)
    def _():
        greet(spot - 2)

    pools = [
        pltpu.make_async_copy(src, dst, pool_sem.at[i])
        for i, (src, dst) in enumerate(((pk_hbm, pk_ref), (pv_hbm, pv_ref)))
    ]
    for copy in pools:
        copy.start()

    def load(i, h):
        src, dst = ((k_hbm, k_buf), (v_hbm, v_buf), (q_hbm, q_buf))[i]
        return pltpu.make_async_copy(src.at[h], dst.at[h], in_sem.at[i, h])

    for h in range(heads):
        load(0, h).start()
        load(1, h).start()
    for h in range(heads):
        load(2, h).start()

    def remote(src, dst, send_sem, recv_sem, to):
        return pltpu.make_async_remote_copy(
            src_ref=src,
            dst_ref=dst,
            send_sem=send_sem,
            recv_sem=recv_sem,
            device_id={"seq": to},
            device_id_type=pl.DeviceIdType.MESH,
        )

    def group(g):
        return pl.ds(g * span, span)

    def ask(g, to):
        src = q_hbm.at[group(g), pl.ds(0, block), :]
        return remote(src, asked.at[group(g)], ask_send.at[g], ask_recv.at[g], to)

    def give(g, to):
        src, dst = answer.at[group(g)], back.at[group(g)]
        return remote(src, dst, back_send.at[g], back_recv.at[g], to)

    def give_stat(g, to):
        src, dst = stat.at[group(g)], stat_back.at[group(g)]
        return remote(src, dst, stat_sem.at[0, g], stat_sem.at[1, g], to)

    def sum_copy(source, p, to):
        at = summ.at[source, pl.ds(p * step, step)]
        return remote(at, at, sum_send.at[source, p], sum_recv.at[source, p], to)

    def skip_copy(p):
        at = summ.at[spot, pl.ds(p * step, step)]
        return remote(at, at, skip_send.at[p], sum_recv.at[spot, p], spot + 2)

    def enter():
        known = (has_prev, has_next, has_skip)
        pl.semaphore_wait(barrier, sum(jnp.where(one, 1, 0) for one in known))

    def send_asks():
        @pl.when(has_prev)
        def _():
            for g in range(chunks):
                ask(g, spot - 1).start()

    def region(body):
        pl.when(spot >= 0)(body)

    def heads_of(g):
        return [g * span + i for i in range(span)]

    def parts_of(g):
        return range(g * span // step, (g + 1) * span // step)

    def span_of(b, n=1):
        return pl.ds(b * block, n * block)

    @pl.when(jnp.logical_not(has_next))
    def _():
        enter()
        send_asks()

    for copy in pools:
        copy.wait()
    for g in range(chunks):
        for h in heads_of(g):
            load(0, h).wait()
            load(1, h).wait()
        for h in heads_of(g):
            for which, (pool, buf) in enumerate(((pk_ref, k_buf), (pv_ref, v_buf))):
                parts = [dot(pool[h], buf[h, span_of(b), :]) for b in range(blocks)]
                summ[spot, h, which] = jnp.concatenate(parts, axis=0).astype(BF16)

        @pl.when(has_next)
        def _():
            if g == 0:
                enter()
            for p in parts_of(g):
                sum_copy(spot, p, spot + 1).start()

            @pl.when(has_skip)
            def _():
                for p in parts_of(g):
                    skip_copy(p).start()

            if g == 0:
                send_asks()

    def clear(i, c):
        summ[i] = jnp.zeros(summ.shape[1:], BF16)
        return c

    lax.fori_loop(spot + 1, slots, clear, 0)

    @pl.when(spot == 0)
    def _():
        back[...] = jnp.zeros(back.shape, BF16)
        top_row = lax.broadcasted_iota(jnp.int32, stat_back.shape, 1) == 0
        stat_back[...] = jnp.where(top_row, NEG, 0.0)

    key_at = lax.broadcasted_iota(jnp.int32, (block, block), 0)
    query_at = lax.broadcasted_iota(jnp.int32, (block, block), 1)
    here = key_at <= query_at

    def soften(scores):
        top = jnp.max(scores, axis=0, keepdims=True)
        return top, jnp.exp2((scores - top) * gain)

    def near(g):
        @region
        def _():
            for h in heads_of(g):
                for b in range(blocks):
                    q = q_buf[h, span_of(b), :]
                    if b:
                        scores = dot_t(k_buf[h, span_of(b - 1, 2), :], q)
                        scores = jnp.where(here, scores[block:], scores[:block])
                    else:
                        scores = jnp.where(here, dot_t(k_buf[h, span_of(b), :], q), NEG)
                    top, weights = soften(scores)
                    top_s[h, :, span_of(b)] = top
                    total_s[h, :, span_of(b)] = jnp.sum(weights, axis=0, keepdims=True)
                    acc_s[h, :, span_of(b)] = weights

        @region
        def _():
            for h in heads_of(g):
                vt = jnp.transpose(v_buf[h])
                last_vt[h] = vt[:, rows - block :]
                for b in range(blocks):
                    weights = acc_s[h, :, span_of(b)]
                    both = jnp.where(here, weights, 0.0).astype(BF16)
                    if b:
                        before = jnp.where(here, 0.0, weights).astype(BF16)
                        both = jnp.concatenate([before, both], axis=0)
                    acc_s[h, :, span_of(b)] = dot(vt[:, max(b - 1, 0) * block : (b + 1) * block], both)

    def respond(g):
        @pl.when(has_next)
        def _():
            ask(g, spot).wait_recv()
            scores = [dot_t(k_buf[h, span_of(blocks - 1), :], asked[h]) for h in heads_of(g)]
            for h, s in zip(heads_of(g), scores):
                top, weights = soften(jnp.where(here, NEG, s))
                weights = jnp.where(here, 0.0, weights)
                stat[h] = jnp.concatenate([top, jnp.sum(weights, axis=0, keepdims=True)], axis=0)
                answer[h] = dot(last_vt[h], weights.astype(BF16)).astype(BF16)
            give_stat(g, spot + 1).start()
            give(g, spot + 1).start()

    def forwards(d):
        first = jnp.logical_or(even, d != 1)
        return jnp.logical_and(has_next, jnp.logical_and(spot >= d, first))

    def relay(g, d):
        @pl.when(forwards(d))
        def _():
            for p in parts_of(g):
                sum_copy(spot - d, p, spot).wait_recv()
                sum_copy(spot - d, p, spot + 1).start()

    def relay_rest(d, c):
        for g in range(chunks):
            relay(g, d)
        return c

    def land(g):
        def one(d, c):
            @pl.when(jnp.logical_not(forwards(d)))
            def _():
                for p in parts_of(g):
                    sum_copy(spot - d, p, spot).wait_recv()

            return c

        lax.fori_loop(1, spot + 1, one, 0)

    def far_weights(g, j):
        @region
        def _():
            for h in heads_of(g):
                keys = jnp.concatenate([summ[j * per + i, h, 0] for i in range(per)], axis=0)
                scores = dot_t(keys, q_buf[h])
                for b in range(blocks):
                    limit = (spot * blocks + b) * sums - j * block
                    part = jnp.where(key_at < limit, scores[:, b * block : (b + 1) * block], NEG)
                    old = top_s[h, :, span_of(b)]
                    top = jnp.maximum(old, jnp.max(part, axis=0, keepdims=True))
                    weights = jnp.exp2((part - top) * gain)
                    fade = jnp.exp2((old - top) * gain)
                    top_s[h, :, span_of(b)] = top
                    fade_s[h, :, span_of(b)] = fade
                    total = total_s[h, :, span_of(b)]
                    total_s[h, :, span_of(b)] = total * fade + jnp.sum(weights, axis=0, keepdims=True)
                    far_w[h, :, span_of(b)] = weights.astype(BF16)

    def far_values(g, j, finish):
        @region
        def _():
            for h in heads_of(g):
                values = jnp.concatenate([summ[j * per + i, h, 1] for i in range(per)], axis=0)
                acc = acc_s[h] * fade_s[h] + dot(jnp.transpose(values), far_w[h])
                if finish:
                    acc_s[h, :, :block] = acc[:, :block]
                    write(h, acc)
                else:
                    acc_s[h] = acc

    def write(h, acc):
        out = acc[:, block:] * (1.0 / total_s[h, :, block:])
        o_ref[h, block:, :] = jnp.transpose(out.astype(BF16))

    def far(g):
        if slots == per:
            far_weights(g, 0)
            far_values(g, 0, True)
            return

        def chunk(j, c):
            far_weights(g, j)
            far_values(g, j, False)
            return c

        lax.fori_loop(0, (spot * own + own - sums + block - 1) // block, chunk, 0)

        @region
        def _():
            for h in heads_of(g):
                write(h, acc_s[h])

    def weigh(g):
        @pl.when(has_prev)
        def _():
            give_stat(g, spot).wait_recv()

        @region
        def _():
            for h in heads_of(g):
                old, new = top_s[h, :, :block], stat_back[h, 0:1, :]
                top = jnp.maximum(old, new)
                fade, new_fade = jnp.exp2((old - top) * gain), jnp.exp2((new - top) * gain)
                total = total_s[h, :, :block] * fade + stat_back[h, 1:2, :] * new_fade
                share = 1.0 / total
                fade_s[h, :, :block] = new_fade * share
                acc_s[h, :, :block] = acc_s[h, :, :block] * (fade * share)

    def merge(g):
        @pl.when(has_prev)
        def _():
            give(g, spot).wait_recv()

        @region
        def _():
            for h in heads_of(g):
                out = acc_s[h, :, :block] + back[h].astype(F32) * fade_s[h, :, :block]
                o_ref[h, :block, :] = jnp.transpose(out.astype(BF16))

    for h in range(heads):
        load(2, h).wait()
    for g in range(chunks):
        near(g)
    for g in range(chunks):
        relay(g, 1)
        relay(g, 2)
        respond(g)
    lax.fori_loop(3, spot + 1, relay_rest, 0)
    for g in range(chunks):
        land(g)
        far(g)
    for g in range(chunks):
        weigh(g)
        merge(g)

    @pl.when(has_prev)
    def _():
        for g in range(chunks):
            ask(g, spot - 1).wait_send()

    @pl.when(has_next)
    def _():
        for g in range(chunks):
            give(g, spot + 1).wait_send()
            give_stat(g, spot + 1).wait_send()

        for p in range(heads // step):
            sum_copy(spot, p, spot + 1).wait_send()

        @pl.when(has_skip)
        def _():
            for p in range(heads // step):
                skip_copy(p).wait_send()

        def sent(d, c):
            @pl.when(forwards(d))
            def _():
                for p in range(heads // step):
                    sum_copy(spot - d, p, spot + 1).wait_send()

            return c

        lax.fori_loop(1, spot + 1, sent, 0)


def on_device(peers, queries, keys, values, pool_keys, pool_values):
    rows, heads, width = queries.shape
    sums, block = pool_keys.shape[1], pool_keys.shape[2]
    own = rows // block * sums
    per = block // own
    slots = -(-peers // per) * per
    span = next(n for n in (3, 2, 1) if heads % n == 0)
    step = span
    chunks = heads // span
    q, k, v = (jnp.moveaxis(x, 1, 0) for x in (queries, keys, values))
    hbm = pl.BlockSpec(memory_space=pltpu.HBM)
    out = pl.pallas_call(
        functools.partial(kernel, peers, span, step),
        out_shape=pltpu.VMEM((heads, rows, width), BF16),
        in_specs=[hbm] * 5,
        out_specs=pl.BlockSpec(memory_space=pltpu.VMEM),
        scratch_shapes=[
            pltpu.VMEM((heads, rows, width), BF16),
            pltpu.VMEM((heads, rows, width), BF16),
            pltpu.VMEM((heads, rows, width), BF16),
            pltpu.VMEM(pool_keys.shape, BF16),
            pltpu.VMEM(pool_values.shape, BF16),
            pltpu.VMEM((heads, width, block), BF16),
            pltpu.VMEM((heads, block, width), BF16),
            pltpu.VMEM((heads, width, block), BF16),
            pltpu.VMEM((heads, width, block), BF16),
            pltpu.VMEM((heads, 2, block), F32),
            pltpu.VMEM((heads, 2, block), F32),
            pltpu.VMEM((slots, heads, 2, own, width), BF16),
            pltpu.VMEM((heads, 1, rows), F32),
            pltpu.VMEM((heads, 1, rows), F32),
            pltpu.VMEM((heads, 1, rows), F32),
            pltpu.VMEM((heads, width, rows), F32),
            pltpu.VMEM((heads, block, rows), BF16),
            pltpu.SemaphoreType.DMA((3, heads)),
            pltpu.SemaphoreType.DMA((2,)),
            pltpu.SemaphoreType.DMA((chunks,)),
            pltpu.SemaphoreType.DMA((chunks,)),
            pltpu.SemaphoreType.DMA((chunks,)),
            pltpu.SemaphoreType.DMA((chunks,)),
            pltpu.SemaphoreType.DMA((2, chunks)),
            pltpu.SemaphoreType.DMA((slots, heads // step)),
            pltpu.SemaphoreType.DMA((slots, heads // step)),
            pltpu.SemaphoreType.DMA((heads // step,)),
        ],
        compiler_params=pltpu.CompilerParams(
            collective_id=0, has_side_effects=True, vmem_limit_bytes=40 * 1024 * 1024
        ),
    )(*(pltpu.with_memory_space_constraint(x, pltpu.HBM) for x in (q, k, v, pool_keys, pool_values)))
    return jnp.moveaxis(out, 0, 1)


def solution(mesh):
    in_specs = (
        P(("groups", "seq"), "heads", None),
        P(("groups", "seq"), "heads", None),
        P(("groups", "seq"), "heads", None),
        P("heads", None, None),
        P("heads", None, None),
    )
    out_specs = P(("groups", "seq"), "heads", None)
    return jax.shard_map(
        functools.partial(on_device, mesh.shape["seq"]),
        mesh=mesh, in_specs=in_specs, out_specs=out_specs, check_vma=False,
    )
```

```python
import functools
import math

import jax
import jax.numpy as jnp
from jax import lax
from jax.experimental import pallas as pl
from jax.experimental.pallas import tpu as pltpu
from jax.sharding import PartitionSpec as P

NEG = -1e30
F32 = jnp.float32
BF16 = jnp.bfloat16


def dot_t(a, b):
    return lax.dot_general(a, b, (((1,), (1,)), ((), ())), preferred_element_type=F32)


def dot(a, b):
    return jnp.dot(a, b, preferred_element_type=F32)


def kernel(
    peers, span, step, q_hbm, k_hbm, v_hbm, pk_hbm, pv_hbm, o_ref,
    q_buf, k_buf, v_buf, pk_ref, pv_ref, last_vt, asked, answer, back, stat, stat_back,
    summ, top_s, total_s, fade_s, acc_s, far_w,
    in_sem, pool_sem, ask_send, ask_recv, back_send, back_recv, stat_sem, sum_send, sum_recv, skip_send,
):
    heads, rows, width = q_buf.shape
    sums, block = pk_ref.shape[1], pk_ref.shape[2]
    blocks = rows // block
    own = blocks * sums
    per = block // own
    slots = summ.shape[0]
    chunks = heads // span
    gain = (width ** -0.5) * math.log2(math.e)
    spot = lax.axis_index("seq")
    has_next = spot < peers - 1
    has_prev = spot > 0
    even = lax.rem(spot, 2) == 0
    late = jnp.logical_and(spot == peers - 2, lax.rem(lax.axis_index("heads"), 2) == 1)
    has_skip = jnp.logical_and(even, spot < peers - 2)
    from_skip = jnp.logical_and(even, spot > 1)

    barrier = pltpu.get_barrier_semaphore()

    def greet(to):
        pl.semaphore_signal(
            barrier, inc=1, device_id={"seq": to}, device_id_type=pl.DeviceIdType.MESH
        )

    @pl.when(has_prev)
    def _():
        greet(spot - 1)

    @pl.when(has_next)
    def _():
        greet(spot + 1)

    @pl.when(from_skip)
    def _():
        greet(spot - 2)

    pools = [
        pltpu.make_async_copy(src, dst, pool_sem.at[i])
        for i, (src, dst) in enumerate(((pk_hbm, pk_ref), (pv_hbm, pv_ref)))
    ]
    for copy in pools:
        copy.start()

    def load(i, h):
        src, dst = ((k_hbm, k_buf), (v_hbm, v_buf), (q_hbm, q_buf))[i]
        return pltpu.make_async_copy(src.at[h], dst.at[h], in_sem.at[i, h])

    for h in range(heads):
        load(0, h).start()
        load(1, h).start()
    for h in range(heads):
        load(2, h).start()

    def remote(src, dst, send_sem, recv_sem, to):
        return pltpu.make_async_remote_copy(
            src_ref=src,
            dst_ref=dst,
            send_sem=send_sem,
            recv_sem=recv_sem,
            device_id={"seq": to},
            device_id_type=pl.DeviceIdType.MESH,
        )

    def group(g):
        return pl.ds(g * span, span)

    def ask(g, to):
        src = q_hbm.at[group(g), pl.ds(0, block), :]
        return remote(src, asked.at[group(g)], ask_send.at[g], ask_recv.at[g], to)

    def give(g, to):
        src, dst = answer.at[group(g)], back.at[group(g)]
        return remote(src, dst, back_send.at[g], back_recv.at[g], to)

    def give_stat(g, to):
        src, dst = stat.at[group(g)], stat_back.at[group(g)]
        return remote(src, dst, stat_sem.at[0, g], stat_sem.at[1, g], to)

    def sum_copy(source, p, to):
        at = summ.at[source, pl.ds(p * step, step)]
        return remote(at, at, sum_send.at[source, p], sum_recv.at[source, p], to)

    def skip_copy(p):
        at = summ.at[spot, pl.ds(p * step, step)]
        return remote(at, at, skip_send.at[p], sum_recv.at[spot, p], spot + 2)

    def enter():
        known = (has_prev, has_next, has_skip)
        pl.semaphore_wait(barrier, sum(jnp.where(one, 1, 0) for one in known))

    def send_asks():
        @pl.when(has_prev)
        def _():
            for g in range(chunks):
                ask(g, spot - 1).start()

    def region(body):
        pl.when(spot >= 0)(body)

    def heads_of(g):
        return [g * span + i for i in range(span)]

    def parts_of(g):
        return range(g * span // step, (g + 1) * span // step)

    def span_of(b, n=1):
        return pl.ds(b * block, n * block)

    @pl.when(jnp.logical_not(has_next))
    def _():
        enter()
        send_asks()

    for copy in pools:
        copy.wait()
    for g in range(chunks):
        for h in heads_of(g):
            load(0, h).wait()
            load(1, h).wait()
        for h in heads_of(g):
            for which, (pool, buf) in enumerate(((pk_ref, k_buf), (pv_ref, v_buf))):
                parts = [dot(pool[h], buf[h, span_of(b), :]) for b in range(blocks)]
                summ[spot, h, which] = jnp.concatenate(parts, axis=0).astype(BF16)

        @pl.when(has_next)
        def _():
            if g == 0:
                enter()
            for p in parts_of(g):
                sum_copy(spot, p, spot + 1).start()

            @pl.when(has_skip)
            def _():
                for p in parts_of(g):
                    skip_copy(p).start()

            if g == 0:
                send_asks()

    def clear(i, c):
        summ[i] = jnp.zeros(summ.shape[1:], BF16)
        return c

    lax.fori_loop(spot + 1, slots, clear, 0)

    @pl.when(spot == 0)
    def _():
        back[...] = jnp.zeros(back.shape, BF16)
        top_row = lax.broadcasted_iota(jnp.int32, stat_back.shape, 1) == 0
        stat_back[...] = jnp.where(top_row, NEG, 0.0)

    key_at = lax.broadcasted_iota(jnp.int32, (block, block), 0)
    query_at = lax.broadcasted_iota(jnp.int32, (block, block), 1)
    here = key_at <= query_at

    def soften(scores):
        top = jnp.max(scores, axis=0, keepdims=True)
        return top, jnp.exp2((scores - top) * gain)

    def near(g):
        @region
        def _():
            for h in heads_of(g):
                for b in range(blocks):
                    q = q_buf[h, span_of(b), :]
                    if b:
                        scores = dot_t(k_buf[h, span_of(b - 1, 2), :], q)
                        scores = jnp.where(here, scores[block:], scores[:block])
                    else:
                        scores = jnp.where(here, dot_t(k_buf[h, span_of(b), :], q), NEG)
                    top, weights = soften(scores)
                    top_s[h, :, span_of(b)] = top
                    total_s[h, :, span_of(b)] = jnp.sum(weights, axis=0, keepdims=True)
                    acc_s[h, :, span_of(b)] = weights

        @region
        def _():
            for h in heads_of(g):
                vt = jnp.transpose(v_buf[h])
                last_vt[h] = vt[:, rows - block :]
                for b in range(blocks):
                    weights = acc_s[h, :, span_of(b)]
                    both = jnp.where(here, weights, 0.0).astype(BF16)
                    if b:
                        before = jnp.where(here, 0.0, weights).astype(BF16)
                        both = jnp.concatenate([before, both], axis=0)
                    acc_s[h, :, span_of(b)] = dot(vt[:, max(b - 1, 0) * block : (b + 1) * block], both)

    def respond(g):
        @pl.when(has_next)
        def _():
            ask(g, spot).wait_recv()
            scores = [dot_t(k_buf[h, span_of(blocks - 1), :], asked[h]) for h in heads_of(g)]
            for h, s in zip(heads_of(g), scores):
                top, weights = soften(jnp.where(here, NEG, s))
                weights = jnp.where(here, 0.0, weights)
                stat[h] = jnp.concatenate([top, jnp.sum(weights, axis=0, keepdims=True)], axis=0)
                answer[h] = dot(last_vt[h], weights.astype(BF16)).astype(BF16)

    def hand_over(g):
        give(g, spot + 1).start()
        give_stat(g, spot + 1).start()

    def forwards(d):
        first = jnp.logical_or(even, d != 1)
        return jnp.logical_and(has_next, jnp.logical_and(spot >= d, first))

    def relay(g, d):
        @pl.when(forwards(d))
        def _():
            for p in parts_of(g):
                sum_copy(spot - d, p, spot).wait_recv()
                sum_copy(spot - d, p, spot + 1).start()

    def relay_rest(d, c):
        for g in range(chunks):
            relay(g, d)
        return c

    def land(g):
        def one(d, c):
            @pl.when(jnp.logical_not(forwards(d)))
            def _():
                for p in parts_of(g):
                    sum_copy(spot - d, p, spot).wait_recv()

            return c

        lax.fori_loop(1, spot + 1, one, 0)

    def far_weights(g, j):
        @region
        def _():
            for h in heads_of(g):
                keys = jnp.concatenate([summ[j * per + i, h, 0] for i in range(per)], axis=0)
                scores = dot_t(keys, q_buf[h])
                for b in range(blocks):
                    limit = (spot * blocks + b) * sums - j * block
                    part = jnp.where(key_at < limit, scores[:, b * block : (b + 1) * block], NEG)
                    old = top_s[h, :, span_of(b)]
                    top = jnp.maximum(old, jnp.max(part, axis=0, keepdims=True))
                    weights = jnp.exp2((part - top) * gain)
                    fade = jnp.exp2((old - top) * gain)
                    top_s[h, :, span_of(b)] = top
                    fade_s[h, :, span_of(b)] = fade
                    total = total_s[h, :, span_of(b)]
                    total_s[h, :, span_of(b)] = total * fade + jnp.sum(weights, axis=0, keepdims=True)
                    far_w[h, :, span_of(b)] = weights.astype(BF16)

    def far_values(g, j, finish):
        @region
        def _():
            for h in heads_of(g):
                values = jnp.concatenate([summ[j * per + i, h, 1] for i in range(per)], axis=0)
                acc = acc_s[h] * fade_s[h] + dot(jnp.transpose(values), far_w[h])
                if finish:
                    acc_s[h, :, :block] = acc[:, :block]
                    write(h, acc)
                else:
                    acc_s[h] = acc

    def write(h, acc):
        out = acc[:, block:] * (1.0 / total_s[h, :, block:])
        o_ref[h, block:, :] = jnp.transpose(out.astype(BF16))

    def far(g):
        if slots == per:
            far_weights(g, 0)
            far_values(g, 0, True)
            return

        def chunk(j, c):
            far_weights(g, j)
            far_values(g, j, False)
            return c

        lax.fori_loop(0, (spot * own + own - sums + block - 1) // block, chunk, 0)

        @region
        def _():
            for h in heads_of(g):
                write(h, acc_s[h])

    def merge(g):
        @pl.when(has_prev)
        def _():
            give(g, spot).wait_recv()
            give_stat(g, spot).wait_recv()

        @region
        def _():
            for h in heads_of(g):
                old, new = top_s[h, :, :block], stat_back[h, 0:1, :]
                top = jnp.maximum(old, new)
                fade, new_fade = jnp.exp2((old - top) * gain), jnp.exp2((new - top) * gain)
                total = total_s[h, :, :block] * fade + stat_back[h, 1:2, :] * new_fade
                acc = acc_s[h, :, :block] * fade + back[h].astype(F32) * new_fade
                o_ref[h, :block, :] = jnp.transpose((acc * (1.0 / total)).astype(BF16))

    for h in range(heads):
        load(2, h).wait()
    for g in range(chunks):
        near(g)
    for g in range(chunks):
        relay(g, 1)
        relay(g, 2)
        respond(g)
        if g < chunks - 1:
            pl.when(has_next)(lambda: hand_over(g))
        else:
            pl.when(jnp.logical_and(has_next, jnp.logical_not(late)))(lambda: hand_over(g))
    lax.fori_loop(3, spot + 1, relay_rest, 0)
    for g in range(chunks):
        land(g)
        far(g)
    for g in range(chunks):
        merge(g)
        if g == 0:
            pl.when(late)(lambda: hand_over(chunks - 1))

    @pl.when(has_prev)
    def _():
        for g in range(chunks):
            ask(g, spot - 1).wait_send()

    @pl.when(has_next)
    def _():
        for g in range(chunks):
            give(g, spot + 1).wait_send()
            give_stat(g, spot + 1).wait_send()

        for p in range(heads // step):
            sum_copy(spot, p, spot + 1).wait_send()

        @pl.when(has_skip)
        def _():
            for p in range(heads // step):
                skip_copy(p).wait_send()

        def sent(d, c):
            @pl.when(forwards(d))
            def _():
                for p in range(heads // step):
                    sum_copy(spot - d, p, spot + 1).wait_send()

            return c

        lax.fori_loop(1, spot + 1, sent, 0)


def on_device(peers, queries, keys, values, pool_keys, pool_values):
    rows, heads, width = queries.shape
    sums, block = pool_keys.shape[1], pool_keys.shape[2]
    own = rows // block * sums
    per = block // own
    slots = -(-peers // per) * per
    span = next(n for n in (3, 2, 1) if heads % n == 0)
    step = span
    chunks = heads // span
    q, k, v = (jnp.moveaxis(x, 1, 0) for x in (queries, keys, values))
    hbm = pl.BlockSpec(memory_space=pltpu.HBM)
    out = pl.pallas_call(
        functools.partial(kernel, peers, span, step),
        out_shape=pltpu.VMEM((heads, rows, width), BF16),
        in_specs=[hbm] * 5,
        out_specs=pl.BlockSpec(memory_space=pltpu.VMEM),
        scratch_shapes=[
            pltpu.VMEM((heads, rows, width), BF16),
            pltpu.VMEM((heads, rows, width), BF16),
            pltpu.VMEM((heads, rows, width), BF16),
            pltpu.VMEM(pool_keys.shape, BF16),
            pltpu.VMEM(pool_values.shape, BF16),
            pltpu.VMEM((heads, width, block), BF16),
            pltpu.VMEM((heads, block, width), BF16),
            pltpu.VMEM((heads, width, block), BF16),
            pltpu.VMEM((heads, width, block), BF16),
            pltpu.VMEM((heads, 2, block), F32),
            pltpu.VMEM((heads, 2, block), F32),
            pltpu.VMEM((slots, heads, 2, own, width), BF16),
            pltpu.VMEM((heads, 1, rows), F32),
            pltpu.VMEM((heads, 1, rows), F32),
            pltpu.VMEM((heads, 1, rows), F32),
            pltpu.VMEM((heads, width, rows), F32),
            pltpu.VMEM((heads, block, rows), BF16),
            pltpu.SemaphoreType.DMA((3, heads)),
            pltpu.SemaphoreType.DMA((2,)),
            pltpu.SemaphoreType.DMA((chunks,)),
            pltpu.SemaphoreType.DMA((chunks,)),
            pltpu.SemaphoreType.DMA((chunks,)),
            pltpu.SemaphoreType.DMA((chunks,)),
            pltpu.SemaphoreType.DMA((2, chunks)),
            pltpu.SemaphoreType.DMA((slots, heads // step)),
            pltpu.SemaphoreType.DMA((slots, heads // step)),
            pltpu.SemaphoreType.DMA((heads // step,)),
        ],
        compiler_params=pltpu.CompilerParams(
            collective_id=0, has_side_effects=True, vmem_limit_bytes=40 * 1024 * 1024
        ),
    )(*(pltpu.with_memory_space_constraint(x, pltpu.HBM) for x in (q, k, v, pool_keys, pool_values)))
    return jnp.moveaxis(out, 0, 1)


def solution(mesh):
    in_specs = (
        P(("groups", "seq"), "heads", None),
        P(("groups", "seq"), "heads", None),
        P(("groups", "seq"), "heads", None),
        P("heads", None, None),
        P("heads", None, None),
    )
    out_specs = P(("groups", "seq"), "heads", None)
    return jax.shard_map(
        functools.partial(on_device, mesh.shape["seq"]),
        mesh=mesh, in_specs=in_specs, out_specs=out_specs, check_vma=False,
    )
```

```python
import functools
import math

import jax
import jax.numpy as jnp
from jax import lax
from jax.experimental import pallas as pl
from jax.experimental.pallas import tpu as pltpu
from jax.sharding import PartitionSpec as P

NEG = -1e30
F32 = jnp.float32
BF16 = jnp.bfloat16


def dot_t(a, b):
    return lax.dot_general(a, b, (((1,), (1,)), ((), ())), preferred_element_type=F32)


def dot(a, b):
    return jnp.dot(a, b, preferred_element_type=F32)


def kernel(
    peers, span, step, q_hbm, k_hbm, v_hbm, pk_hbm, pv_hbm, o_ref,
    q_buf, k_buf, v_buf, pk_ref, pv_ref, last_vt, asked, answer, back, stat, stat_back,
    summ, top_s, total_s, fade_s, acc_s, far_w,
    in_sem, pool_sem, ask_send, ask_recv, back_send, back_recv, stat_sem, sum_send, sum_recv, skip_send,
):
    heads, rows, width = q_buf.shape
    sums, block = pk_ref.shape[1], pk_ref.shape[2]
    blocks = rows // block
    own = blocks * sums
    per = block // own
    slots = summ.shape[0]
    chunks = heads // span
    gain = (width ** -0.5) * math.log2(math.e)
    spot = lax.axis_index("seq")
    has_next = spot < peers - 1
    has_prev = spot > 0
    even = lax.rem(spot, 2) == 0
    has_skip = jnp.logical_and(even, spot < peers - 2)
    from_skip = jnp.logical_and(even, spot > 1)

    barrier = pltpu.get_barrier_semaphore()

    def greet(to):
        pl.semaphore_signal(
            barrier, inc=1, device_id={"seq": to}, device_id_type=pl.DeviceIdType.MESH
        )

    @pl.when(has_prev)
    def _():
        greet(spot - 1)

    @pl.when(has_next)
    def _():
        greet(spot + 1)

    @pl.when(from_skip)
    def _():
        greet(spot - 2)

    pools = [
        pltpu.make_async_copy(src, dst, pool_sem.at[i])
        for i, (src, dst) in enumerate(((pk_hbm, pk_ref), (pv_hbm, pv_ref)))
    ]
    for copy in pools:
        copy.start()

    def load(i, h):
        src, dst = ((k_hbm, k_buf), (v_hbm, v_buf), (q_hbm, q_buf))[i]
        return pltpu.make_async_copy(src.at[h], dst.at[h], in_sem.at[i, h])

    for h in range(heads):
        load(0, h).start()
        load(1, h).start()
    for h in range(heads):
        load(2, h).start()

    def remote(src, dst, send_sem, recv_sem, to):
        return pltpu.make_async_remote_copy(
            src_ref=src,
            dst_ref=dst,
            send_sem=send_sem,
            recv_sem=recv_sem,
            device_id={"seq": to},
            device_id_type=pl.DeviceIdType.MESH,
        )

    def group(g):
        return pl.ds(g * span, span)

    def ask(g, to):
        src = q_hbm.at[group(g), pl.ds(0, block), :]
        return remote(src, asked.at[group(g)], ask_send.at[g], ask_recv.at[g], to)

    def give(g, to):
        src, dst = answer.at[group(g)], back.at[group(g)]
        return remote(src, dst, back_send.at[g], back_recv.at[g], to)

    def give_stat(g, to):
        src, dst = stat.at[group(g)], stat_back.at[group(g)]
        return remote(src, dst, stat_sem.at[0, g], stat_sem.at[1, g], to)

    def sum_copy(source, p, to):
        at = summ.at[source, pl.ds(p * step, step)]
        return remote(at, at, sum_send.at[source, p], sum_recv.at[source, p], to)

    def skip_copy(p):
        at = summ.at[spot, pl.ds(p * step, step)]
        return remote(at, at, skip_send.at[p], sum_recv.at[spot, p], spot + 2)

    def enter():
        known = (has_prev, has_next, has_skip)
        pl.semaphore_wait(barrier, sum(jnp.where(one, 1, 0) for one in known))

    def send_asks():
        @pl.when(has_prev)
        def _():
            for g in range(chunks):
                ask(g, spot - 1).start()

    def region(body):
        pl.when(spot >= 0)(body)

    def heads_of(g):
        return [g * span + i for i in range(span)]

    def parts_of(g):
        return range(g * span // step, (g + 1) * span // step)

    def span_of(b, n=1):
        return pl.ds(b * block, n * block)

    @pl.when(jnp.logical_not(has_next))
    def _():
        enter()
        send_asks()

    for copy in pools:
        copy.wait()
    for g in range(chunks):
        for h in heads_of(g):
            load(0, h).wait()
            load(1, h).wait()
        for h in heads_of(g):
            for which, (pool, buf) in enumerate(((pk_ref, k_buf), (pv_ref, v_buf))):
                parts = [dot(pool[h], buf[h, span_of(b), :]) for b in range(blocks)]
                summ[spot, h, which] = jnp.concatenate(parts, axis=0).astype(BF16)

        @pl.when(has_next)
        def _():
            if g == 0:
                enter()
            for p in parts_of(g):
                sum_copy(spot, p, spot + 1).start()

            @pl.when(has_skip)
            def _():
                for p in parts_of(g):
                    skip_copy(p).start()

            if g == 0:
                send_asks()

    def clear(i, c):
        summ[i] = jnp.zeros(summ.shape[1:], BF16)
        return c

    lax.fori_loop(spot + 1, slots, clear, 0)

    @pl.when(spot == 0)
    def _():
        back[...] = jnp.zeros(back.shape, BF16)
        top_row = lax.broadcasted_iota(jnp.int32, stat_back.shape, 1) == 0
        stat_back[...] = jnp.where(top_row, NEG, 0.0)

    key_at = lax.broadcasted_iota(jnp.int32, (block, block), 0)
    query_at = lax.broadcasted_iota(jnp.int32, (block, block), 1)
    here = key_at <= query_at

    def soften(scores):
        top = jnp.max(scores, axis=0, keepdims=True)
        return top, jnp.exp2((scores - top) * gain)

    def near(g):
        @region
        def _():
            for h in heads_of(g):
                for b in range(blocks):
                    q = q_buf[h, span_of(b), :]
                    if b:
                        scores = dot_t(k_buf[h, span_of(b - 1, 2), :], q)
                        scores = jnp.where(here, scores[block:], scores[:block])
                    else:
                        scores = jnp.where(here, dot_t(k_buf[h, span_of(b), :], q), NEG)
                    top, weights = soften(scores)
                    top_s[h, :, span_of(b)] = top
                    total_s[h, :, span_of(b)] = jnp.sum(weights, axis=0, keepdims=True)
                    acc_s[h, :, span_of(b)] = weights

        @region
        def _():
            for h in heads_of(g):
                vt = jnp.transpose(v_buf[h])
                last_vt[h] = vt[:, rows - block :]
                for b in range(blocks):
                    weights = acc_s[h, :, span_of(b)]
                    both = jnp.where(here, weights, 0.0).astype(BF16)
                    if b:
                        before = jnp.where(here, 0.0, weights).astype(BF16)
                        both = jnp.concatenate([before, both], axis=0)
                    acc_s[h, :, span_of(b)] = dot(vt[:, max(b - 1, 0) * block : (b + 1) * block], both)

    def respond(g):
        @pl.when(has_next)
        def _():
            ask(g, spot).wait_recv()
            scores = [dot_t(k_buf[h, span_of(blocks - 1), :], asked[h]) for h in heads_of(g)]
            for h, s in zip(heads_of(g), scores):
                top, weights = soften(jnp.where(here, NEG, s))
                weights = jnp.where(here, 0.0, weights)
                stat[h] = jnp.concatenate([top, jnp.sum(weights, axis=0, keepdims=True)], axis=0)
                answer[h] = dot(last_vt[h], weights.astype(BF16)).astype(BF16)
            give(g, spot + 1).start()
            give_stat(g, spot + 1).start()

    def forwards(d):
        first = jnp.logical_or(even, d != 1)
        return jnp.logical_and(has_next, jnp.logical_and(spot >= d, first))

    def relay(g, d):
        @pl.when(forwards(d))
        def _():
            for p in parts_of(g):
                sum_copy(spot - d, p, spot).wait_recv()
                sum_copy(spot - d, p, spot + 1).start()

    def relay_rest(d, c):
        for g in range(chunks):
            relay(g, d)
        return c

    def land(g):
        def one(d, c):
            @pl.when(jnp.logical_not(forwards(d)))
            def _():
                for p in parts_of(g):
                    sum_copy(spot - d, p, spot).wait_recv()

            return c

        lax.fori_loop(1, spot + 1, one, 0)

    def far_weights(g, j):
        @region
        def _():
            for h in heads_of(g):
                keys = jnp.concatenate([summ[j * per + i, h, 0] for i in range(per)], axis=0)
                scores = dot_t(keys, q_buf[h])
                for b in range(blocks):
                    limit = (spot * blocks + b) * sums - j * block
                    part = jnp.where(key_at < limit, scores[:, b * block : (b + 1) * block], NEG)
                    old = top_s[h, :, span_of(b)]
                    top = jnp.maximum(old, jnp.max(part, axis=0, keepdims=True))
                    weights = jnp.exp2((part - top) * gain)
                    fade = jnp.exp2((old - top) * gain)
                    top_s[h, :, span_of(b)] = top
                    fade_s[h, :, span_of(b)] = fade
                    total = total_s[h, :, span_of(b)]
                    total_s[h, :, span_of(b)] = total * fade + jnp.sum(weights, axis=0, keepdims=True)
                    far_w[h, :, span_of(b)] = weights.astype(BF16)

    def far_values(g, j, finish):
        @region
        def _():
            for h in heads_of(g):
                values = jnp.concatenate([summ[j * per + i, h, 1] for i in range(per)], axis=0)
                acc = acc_s[h] * fade_s[h] + dot(jnp.transpose(values), far_w[h])
                if finish:
                    acc_s[h, :, :block] = acc[:, :block]
                    write(h, acc)
                else:
                    acc_s[h] = acc

    def write(h, acc):
        out = acc[:, block:] * (1.0 / total_s[h, :, block:])
        o_ref[h, block:, :] = jnp.transpose(out.astype(BF16))

    def far(g):
        if slots == per:
            far_weights(g, 0)
            far_values(g, 0, True)
            return

        def chunk(j, c):
            far_weights(g, j)
            far_values(g, j, False)
            return c

        lax.fori_loop(0, (spot * own + own - sums + block - 1) // block, chunk, 0)

        @region
        def _():
            for h in heads_of(g):
                write(h, acc_s[h])

    def merge(g):
        @pl.when(has_prev)
        def _():
            give(g, spot).wait_recv()
            give_stat(g, spot).wait_recv()

        @region
        def _():
            for h in heads_of(g):
                old, new = top_s[h, :, :block], stat_back[h, 0:1, :]
                top = jnp.maximum(old, new)
                fade, new_fade = jnp.exp2((old - top) * gain), jnp.exp2((new - top) * gain)
                total = total_s[h, :, :block] * fade + stat_back[h, 1:2, :] * new_fade
                acc = acc_s[h, :, :block] * fade + back[h].astype(F32) * new_fade
                o_ref[h, :block, :] = jnp.transpose((acc * (1.0 / total)).astype(BF16))

    for h in range(heads):
        load(2, h).wait()
    for g in range(chunks):
        near(g)
    for g in range(chunks):
        relay(g, 1)
        relay(g, 2)
        respond(g)
    lax.fori_loop(3, spot + 1, relay_rest, 0)
    for g in range(chunks):
        land(g)
        far(g)
    for g in range(chunks):
        merge(g)

    @pl.when(has_prev)
    def _():
        for g in range(chunks):
            ask(g, spot - 1).wait_send()

    @pl.when(has_next)
    def _():
        for g in range(chunks):
            give(g, spot + 1).wait_send()
            give_stat(g, spot + 1).wait_send()

        for p in range(heads // step):
            sum_copy(spot, p, spot + 1).wait_send()

        @pl.when(has_skip)
        def _():
            for p in range(heads // step):
                skip_copy(p).wait_send()

        def sent(d, c):
            @pl.when(forwards(d))
            def _():
                for p in range(heads // step):
                    sum_copy(spot - d, p, spot + 1).wait_send()

            return c

        lax.fori_loop(1, spot + 1, sent, 0)


def on_device(peers, queries, keys, values, pool_keys, pool_values):
    rows, heads, width = queries.shape
    sums, block = pool_keys.shape[1], pool_keys.shape[2]
    own = rows // block * sums
    per = block // own
    slots = -(-peers // per) * per
    span = next(n for n in (2, 1) if heads % n == 0)
    step = span
    chunks = heads // span
    q, k, v = (jnp.moveaxis(x, 1, 0) for x in (queries, keys, values))
    hbm = pl.BlockSpec(memory_space=pltpu.HBM)
    out = pl.pallas_call(
        functools.partial(kernel, peers, span, step),
        out_shape=pltpu.VMEM((heads, rows, width), BF16),
        in_specs=[hbm] * 5,
        out_specs=pl.BlockSpec(memory_space=pltpu.VMEM),
        scratch_shapes=[
            pltpu.VMEM((heads, rows, width), BF16),
            pltpu.VMEM((heads, rows, width), BF16),
            pltpu.VMEM((heads, rows, width), BF16),
            pltpu.VMEM(pool_keys.shape, BF16),
            pltpu.VMEM(pool_values.shape, BF16),
            pltpu.VMEM((heads, width, block), BF16),
            pltpu.VMEM((heads, block, width), BF16),
            pltpu.VMEM((heads, width, block), BF16),
            pltpu.VMEM((heads, width, block), BF16),
            pltpu.VMEM((heads, 2, block), F32),
            pltpu.VMEM((heads, 2, block), F32),
            pltpu.VMEM((slots, heads, 2, own, width), BF16),
            pltpu.VMEM((heads, 1, rows), F32),
            pltpu.VMEM((heads, 1, rows), F32),
            pltpu.VMEM((heads, 1, rows), F32),
            pltpu.VMEM((heads, width, rows), F32),
            pltpu.VMEM((heads, block, rows), BF16),
            pltpu.SemaphoreType.DMA((3, heads)),
            pltpu.SemaphoreType.DMA((2,)),
            pltpu.SemaphoreType.DMA((chunks,)),
            pltpu.SemaphoreType.DMA((chunks,)),
            pltpu.SemaphoreType.DMA((chunks,)),
            pltpu.SemaphoreType.DMA((chunks,)),
            pltpu.SemaphoreType.DMA((2, chunks)),
            pltpu.SemaphoreType.DMA((slots, heads // step)),
            pltpu.SemaphoreType.DMA((slots, heads // step)),
            pltpu.SemaphoreType.DMA((heads // step,)),
        ],
        compiler_params=pltpu.CompilerParams(
            collective_id=0, has_side_effects=True, vmem_limit_bytes=40 * 1024 * 1024
        ),
    )(*(pltpu.with_memory_space_constraint(x, pltpu.HBM) for x in (q, k, v, pool_keys, pool_values)))
    return jnp.moveaxis(out, 0, 1)


def solution(mesh):
    in_specs = (
        P(("groups", "seq"), "heads", None),
        P(("groups", "seq"), "heads", None),
        P(("groups", "seq"), "heads", None),
        P("heads", None, None),
        P("heads", None, None),
    )
    out_specs = P(("groups", "seq"), "heads", None)
    return jax.shard_map(
        functools.partial(on_device, mesh.shape["seq"]),
        mesh=mesh, in_specs=in_specs, out_specs=out_specs, check_vma=False,
    )
```
